32 devices in a mesh: dp: 2 (over y), head: 4 (over z), tensor: 4 (over x, core).
Axes of the slice: x: 2, y: 2, z: 4, core: 2. Of those that a mesh axis runs over, the one named last changes fastest.
Arguments:
- tokens: bfloat16 [512, 8192], P('dp', 'tensor'), may hold values from -6 to 6
- cotangent: bfloat16 [512, 8192], P('dp', 'tensor'), may hold values from -6 to 6
- w_gate: bfloat16 [8192, 29568], P('tensor', 'head'), may hold values from -0.0625 to 0.0625
- w_up: bfloat16 [8192, 29568], P('tensor', 'head'), may hold values from -0.0625 to 0.0625
- w_down: bfloat16 [29568, 8192], P('head', 'tensor'), may hold values from -0.03125 to 0.03125
- common_down_factor: bfloat16 [8192, 64], P('tensor'), may hold values from -0.0625 to 0.0625
- head_up: bfloat16 [64, 64, 8192], P('head', None, 'tensor'), may hold values from -0.0625 to 0.0625
- routes: int32 [512, 1], P('dp'), may hold values from 0 to 63
Outputs:
- grad_x: bfloat16 [512, 8192], P(('dp', 'head'), 'tensor')
- grad_shared: float32 [8192, 64], P('tensor')
- up_head_gradients: float32 [64, 64, 8192], P('head', None, 'tensor')
The draws below stay inside these ranges and needn't reach their ends.
Inputs may be any that keep to these rules, and one draw needn't show every extreme that they name: `routes`: each token names one adapter head; the loads are skewed.
All inputs are finite; a program needn't handle non-finite values.
Results may differ from the reference program's by a relative error of at most 0.015.
Values may be sent and summed in bfloat16 or wider, within the bound.
No kernel may reach another device: no remote copies, remote signals or barrier semaphores. Data moves between devices by JAX's collectives and lax.ppermute only.
A program may use at most 256 MiB of HBM per device.

```python
import jax
import jax.numpy as jnp
from jax import lax

MODEL_WIDTH = 8192
FF = 29568
ADAPTER_RANK = 64
UP_HEADS = 64
TOKEN_TOTAL = 512


def levels(key, extent, split, smallest, top_value):
    loudness, own = 1.0, jax.random.fold_in(key, 6)
    for axis_at, blocks in split:
        steps = jnp.exp(jax.random.uniform(jax.random.fold_in(own, axis_at), (blocks,), jnp.float32, smallest / len(split), top_value / len(split)))
        loudness = loudness * jnp.repeat(steps, extent[axis_at] // blocks).reshape([-1 if axis == axis_at else 1 for axis in range(len(extent))])
    return loudness


def choose_distinct(stream_key, rows, number_of, top, lift):
    ranking = jax.random.permutation(jax.random.fold_in(stream_key, 1), number_of)
    boost = ranking
    for power in range(3):
        boost = boost * boost // number_of
    boost = boost * lift // number_of
    lots = jax.random.randint(jax.random.fold_in(stream_key, 2), (rows, number_of), 0, 4096) + boost
    sure = jax.random.permutation(jax.random.fold_in(stream_key, 3), rows)[jnp.arange(number_of) % rows]
    lots = jnp.where(jnp.arange(rows)[:, None] == sure[None, :], 1 << 14, lots)
    merit = lots * number_of + jnp.arange(number_of)
    return lax.top_k(merit.astype(jnp.int32), top)[1].astype(jnp.int32)


def gaussian(rng, shape, scale, most, split=(), held_as=jnp.bfloat16):
    result = jax.random.normal(rng, shape, jnp.float32) * scale
    if len(split) > 0:
        result = levels(rng, shape, split, -0.22, 0.18) * result
    return jnp.clip(result, min=-most, max=most).astype(held_as)


def setup_inputs(seed: int = 0) -> dict:
    keys = jax.random.split(jax.random.key(seed), 9)
    tokens = gaussian(keys[0], (TOKEN_TOTAL, MODEL_WIDTH), 1.0, 6.0, ((0, 2), (1, 4)))
    cotangent = gaussian(keys[1], (TOKEN_TOTAL, MODEL_WIDTH), 1.0, 6.0, ((0, 2), (1, 4)))
    w_gate = gaussian(keys[2], (MODEL_WIDTH, FF), MODEL_WIDTH ** -0.5, 0.0625, ((0, 4), (1, 4)))
    w_up = gaussian(keys[3], (MODEL_WIDTH, FF), MODEL_WIDTH ** -0.5, 0.0625, ((0, 4), (1, 4)))
    w_down = gaussian(keys[4], (FF, MODEL_WIDTH), FF ** -0.5, 0.03125, ((0, 4), (1, 4)))
    common_down_factor = gaussian(keys[5], (MODEL_WIDTH, ADAPTER_RANK), MODEL_WIDTH ** -0.5, 0.0625, ((0, 4),))
    head_up = gaussian(keys[6], (UP_HEADS, ADAPTER_RANK, MODEL_WIDTH), MODEL_WIDTH ** -0.5, 0.0625, ((0, 4), (2, 4)))
    routes = choose_distinct(keys[7], TOKEN_TOTAL, UP_HEADS, 1, 256)
    return {"tokens": tokens, "cotangent": cotangent, "w_gate": w_gate, "w_up": w_up, "w_down": w_down, "common_down_factor": common_down_factor, "head_up": head_up, "routes": routes}


ADAPTER_SCALE = 2.0


def reference(tokens, cotangent, w_gate, w_up, w_down, common_down_factor, head_up, routes):
    gate_preactivation = jnp.dot(tokens, w_gate, preferred_element_type=jnp.float32)
    up_preactivation = jnp.dot(tokens, w_up, preferred_element_type=jnp.float32)
    returned_gradient = jnp.dot(cotangent, w_down.T, preferred_element_type=jnp.float32)
    adapter_selectors = jnp.dot(tokens, common_down_factor, preferred_element_type=jnp.float32).astype(jnp.bfloat16)
    indicator_matrix = (routes == jnp.arange(UP_HEADS, dtype=jnp.int32)[None, :]).astype(jnp.float32)
    head_separated = jnp.dot(cotangent, head_up.reshape(UP_HEADS * ADAPTER_RANK, MODEL_WIDTH).T, preferred_element_type=jnp.float32)
    selector_gradient = (ADAPTER_SCALE * jnp.sum(head_separated.reshape(TOKEN_TOTAL, UP_HEADS, ADAPTER_RANK) * indicator_matrix[:, :, None], axis=1)).astype(jnp.bfloat16)
    sig_gate = jax.nn.sigmoid(gate_preactivation)
    gate_gradient = (returned_gradient * up_preactivation * sig_gate * (1.0 + gate_preactivation * (1.0 - sig_gate))).astype(jnp.bfloat16)
    up_gradient = (returned_gradient * gate_preactivation * sig_gate).astype(jnp.bfloat16)
    grad_x = (jnp.dot(gate_gradient, w_gate.T, preferred_element_type=jnp.float32)
              + jnp.dot(up_gradient, w_up.T, preferred_element_type=jnp.float32)
              + jnp.dot(selector_gradient, common_down_factor.T, preferred_element_type=jnp.float32)).astype(jnp.bfloat16)
    selector_mask = (adapter_selectors.astype(jnp.float32)[:, None, :] * indicator_matrix[:, :, None]).astype(jnp.bfloat16).reshape(TOKEN_TOTAL, UP_HEADS * ADAPTER_RANK)
    up_head_gradients = (ADAPTER_SCALE * jnp.dot(selector_mask.T, cotangent, preferred_element_type=jnp.float32)).reshape(UP_HEADS, ADAPTER_RANK, MODEL_WIDTH)
    grad_shared = jnp.dot(tokens.T, selector_gradient, preferred_element_type=jnp.float32)
    return grad_x, grad_shared, up_head_gradients
```

```python
import jax
import jax.numpy as jnp
from jax import lax
from jax.sharding import PartitionSpec as P

ADAPTER_SCALE = 2.0
CHUNKS = 4
LANE_GROUP = 256
F32, BF16 = jnp.float32, jnp.bfloat16


def contract_last(left, right):
    return lax.dot_general(
        left, right, (((1,), (1,)), ((), ())), preferred_element_type=F32
    )


def contract_first(left, right):
    return lax.dot_general(
        left, right, (((0,), (0,)), ((), ())), preferred_element_type=F32
    )


def chunk_bounds(hidden):
    step = max(hidden // CHUNKS // LANE_GROUP, 1) * LANE_GROUP
    bounds, start = [], 0
    while start < hidden:
        stop = hidden if len(bounds) == CHUNKS - 1 else min(start + step, hidden)
        bounds.append((start, stop))
        start = stop
    return bounds


def local(tokens, cotangent, w_gate, w_up, w_down, common_down_factor, head_up, routes):
    tok_rows, d_cols = tokens.shape
    hidden = w_gate.shape[1]
    rank = common_down_factor.shape[1]
    local_heads = head_up.shape[0]
    n_tensor, n_head, n_dp = (lax.axis_size(a) for a in ("tensor", "head", "dp"))
    chips = n_tensor // 2
    me = lax.axis_index("tensor")
    my_chip, my_core = me // 2, me % 2
    my_head, my_dp = lax.axis_index("head"), lax.axis_index("dp")
    block, half = tok_rows // n_tensor, tok_rows // 2

    def owner(core_step, chip_step):
        core = (my_core + core_step) % 2
        return core * chips + (my_chip + chip_step) % chips

    def relative(rows):
        return jnp.concatenate(
            [
                lax.dynamic_slice_in_dim(rows, owner(a, b) * block, block, 0)
                for a in range(2)
                for b in range(chips)
            ],
            axis=0,
        )

    def swap_core(value):
        return lax.ppermute(value, "tensor", [(i, i ^ 1) for i in range(n_tensor)])

    def shift_chip(value, step):
        pairs = [(i, (i // 2 + step) % chips * 2 + i % 2) for i in range(n_tensor)]
        return lax.ppermute(value, "tensor", pairs)

    def shift(value, axis, count, step):
        return lax.ppermute(value, axis, [(i, (i + step) % count) for i in range(count)])

    def reduce_to_owner(part):
        received = swap_core(part[:, half:])
        total = part[:, :block].astype(F32) + received[:, :block].astype(F32)
        for b in range(1, chips):
            rows = slice(b * block, (b + 1) * block)
            pair = part[:, rows].astype(F32) + received[:, rows].astype(F32)
            total = total + shift_chip(pair.astype(BF16), b).astype(F32)
        return total

    def gather_from_owners(own):
        mine = jnp.concatenate(
            [own] + [shift_chip(own, -b) for b in range(1, chips)], axis=1
        )
        return jnp.concatenate([mine, swap_core(mine)], axis=1)

    tokens = relative(tokens)
    cotangent = relative(cotangent)
    routes = relative(routes)

    other_cotangents = [shift(cotangent, "dp", n_dp, s) for s in range(1, n_dp)]
    other_routes = [shift(routes, "dp", n_dp, s) for s in range(1, n_dp)]

    head_ids = my_head * local_heads + jnp.arange(local_heads, dtype=jnp.int32)[None, :]
    assigned = routes == head_ids
    codes = jnp.dot(tokens, common_down_factor, preferred_element_type=F32)
    separated = contract_last(cotangent, head_up.reshape(local_heads * rank, d_cols))
    code_grad = ADAPTER_SCALE * jnp.sum(
        separated.reshape(tok_rows, local_heads, rank) * assigned.astype(F32)[:, :, None],
        axis=1,
    )
    adapter = reduce_to_owner(jnp.stack([codes, code_grad]).astype(BF16)).astype(BF16)
    own_codes, own_code_grad = adapter[0], adapter[1]
    total = own_code_grad.astype(F32)
    for s in range(1, n_head):
        total = total + shift(own_code_grad, "head", n_head, s).astype(F32)
    adapter = gather_from_owners(jnp.stack([own_codes, total.astype(BF16)]))
    codes, code_grad = adapter[0], adapter[1]

    bounds = chunk_bounds(hidden)
    owned = []
    for start, stop in bounds:
        part = jnp.stack(
            [
                jnp.dot(tokens, w_gate[:, start:stop], preferred_element_type=F32).astype(BF16),
                jnp.dot(tokens, w_up[:, start:stop], preferred_element_type=F32).astype(BF16),
                contract_last(cotangent, w_down[start:stop]).astype(BF16),
            ]
        )
        sums = reduce_to_owner(part)
        gate_pre, up_pre, back = sums[0], sums[1], sums[2]
        sig = jax.nn.sigmoid(gate_pre)
        grad_gate = back * up_pre * sig * (1.0 + gate_pre * (1.0 - sig))
        grad_up = back * gate_pre * sig
        owned.append(jnp.stack([grad_gate, grad_up]).astype(BF16))
    rows = jnp.zeros((tok_rows, d_cols), F32)
    for (start, stop), own in zip(bounds, owned):
        grads = gather_from_owners(own)
        rows = (
            rows
            + contract_last(grads[0], w_gate[:, start:stop])
            + contract_last(grads[1], w_up[:, start:stop])
        )

    def by_group(own, others):
        doubled = jnp.concatenate([own] + others[::-1], axis=0)
        doubled = jnp.concatenate([doubled, doubled], axis=0)
        count = own.shape[0]
        start = (n_dp - my_dp) % n_dp * count
        return lax.dynamic_slice_in_dim(doubled, start, n_dp * count, 0)

    other_codes = [shift(codes, "dp", n_dp, s) for s in range(1, n_dp)]
    all_codes = by_group(codes, other_codes)
    all_routes = by_group(routes, other_routes)
    all_cotangents = by_group(cotangent, other_cotangents)
    masked = jnp.where(
        (all_routes == head_ids)[:, :, None], all_codes[:, None, :], jnp.zeros((), BF16)
    ).reshape(n_dp * tok_rows, local_heads * rank)
    up_heads = ADAPTER_SCALE * contract_first(masked, all_cotangents)
    up_heads = up_heads.reshape(local_heads, rank, d_cols)

    shared = contract_first(tokens, code_grad)
    grad_shared = shared
    for s in range(1, n_dp):
        grad_shared = grad_shared + shift(shared, "dp", n_dp, s)

    rows = rows.astype(BF16)
    out_rows = tok_rows // n_head

    def absolute(values):
        return jnp.concatenate(
            [
                lax.dynamic_slice_in_dim(
                    values,
                    ((k // chips + my_core) % 2 * chips + (k % chips - my_chip) % chips) * block,
                    block,
                    0,
                )
                for k in range(n_tensor)
            ],
            axis=0,
        )

    rows = absolute(rows)
    code_grad = absolute(code_grad)

    def rows_of(values, head):
        return lax.dynamic_slice_in_dim(values, head * out_rows, out_rows, 0)

    grad_x = contract_last(rows_of(code_grad, my_head), common_down_factor)
    grad_x = grad_x + rows_of(rows, my_head).astype(F32)
    for s in range(1, n_head):
        grad_x = grad_x + shift(
            rows_of(rows, (my_head + s) % n_head), "head", n_head, s
        ).astype(F32)
    return grad_x.astype(BF16), grad_shared, up_heads


def solution(mesh):
    placed = (
        P("dp", "tensor"),
        P("dp", "tensor"),
        P("tensor", "head"),
        P("tensor", "head"),
        P("head", "tensor"),
        P("tensor", None),
        P("head", None, "tensor"),
        P("dp", None),
    )
    return jax.shard_map(
        local,
        mesh=mesh,
        in_specs=placed,
        out_specs=(P(("dp", "head"), "tensor"), P("tensor", None), P("head", None, "tensor")),
        check_vma=False,
    )
```

```python
import jax
import jax.numpy as jnp
from jax import lax
from jax.experimental import pallas as pl
from jax.experimental.pallas import tpu as pltpu
from jax.sharding import PartitionSpec as P


ADAPTER_SCALE = 2.0
SHARES = (5, 6, 8, 6, 4)
UNIT = 256
F32, BF16 = jnp.float32, jnp.bfloat16
ANY = pl.BlockSpec(memory_space=pl.ANY)


def contract_last(left, right):
    return lax.dot_general(
        left, right, (((1,), (1,)), ((), ())), preferred_element_type=F32
    )


def contract_first(left, right):
    return lax.dot_general(
        left, right, (((0,), (0,)), ((), ())), preferred_element_type=F32
    )


def chunk_units(hidden):
    units = pl.cdiv(hidden, UNIT)
    total, spans, left, seen = sum(SHARES), [], units, 0
    for share in SHARES:
        seen += share
        first = units - units * seen // total
        if first < left:
            spans.append((first, left - first))
        left = min(left, first)
    return spans


def step_units(span, most):
    first, count = span
    step = most
    while first % step or count % step:
        step //= 2
    return step


def params(limit_mib=48):
    return pltpu.CompilerParams(
        dimension_semantics=("arbitrary",), vmem_limit_bytes=limit_mib * 2**20
    )


def tile_copies(hidden, span, width, weights, buffers, sems):
    first, count = span
    steps = count * UNIT // width
    valid = min(hidden - (first + count) * UNIT + width, width)

    def act(k, step, use):
        def run(units):
            start = pl.multiple_of(first * UNIT + step * width, UNIT)
            use(
                pltpu.make_async_copy(
                    weights[k].at[pl.ds(start, units)],
                    buffers.at[k, step % 2, pl.ds(0, units)],
                    sems.at[k, step % 2],
                )
            )

        if valid == width:
            run(width)
        else:
            pl.when(step < steps - 1)(lambda: run(width))
            pl.when(step == steps - 1)(lambda: run(valid))

    def start(k, step):
        act(k, step, lambda copy: copy.start())

    def wait(k, step):
        act(k, step, lambda copy: copy.wait())

    return start, wait, valid


def keep_valid(value, axis, width, valid, is_last):
    if valid == width:
        return value
    unit = lax.broadcasted_iota(jnp.int32, value.shape, axis)
    return jnp.where(unit < jnp.where(is_last, valid, width), value, jnp.zeros_like(value))


def partial_sums(places, tokens, cotangent, w_gate, w_up, w_down, span, after, extra=None):
    _, count = span
    rows, d_cols = tokens.shape
    hidden = w_gate.shape[0]
    half, n = rows // 2, places.shape[0]
    block = rows // n
    width = step_units(span, 2) * UNIT
    steps = count * UNIT // width
    more = 0 if extra is None else extra.shape[1]

    def kernel(places, *refs):
        sides, weights, refs = refs[:2], refs[2:5], refs[5:]
        kept, sent, held, buffers, row_sems, sems = refs[-6:]
        step = pl.program_id(0)
        start, wait, valid = tile_copies(hidden, span, width, weights, buffers, sems)

        def row_copy(side, k):
            origin = pl.multiple_of(places[k] * block, block)
            return pltpu.make_async_copy(
                sides[side].at[pl.ds(origin, block)],
                held.at[side, pl.ds(k * block, block)],
                row_sems.at[side, k],
            )

        @pl.when(step == 0)
        def _():
            start(0, 0)
            for k in range(n):
                row_copy(0, k).start()
            start(1, 0)
            for k in range(n):
                row_copy(1, k).start()
            start(2, 0)
            for k in range(n):
                row_copy(0, k).wait()

        @pl.when(step < steps)
        def _():
            for k in range(3):
                pl.when(step + 1 < steps)(lambda: start(k, step + 1))
                if k == 2:

                    @pl.when(step == 0)
                    def _():
                        for b in range(n):
                            row_copy(1, b).wait()

                wait(k, step)
                part = contract_last(held[k // 2], buffers[k, step % 2])
                part = keep_valid(part, 1, width, valid, step == steps - 1)
                kept[k] = part[:half].astype(BF16)
                sent[k] = part[half:].astype(BF16)

        if more:

            @pl.when(step == steps)
            def _():
                for k in range(3):
                    value = refs[0][...] if k == 0 else jnp.zeros((rows, more), BF16)
                    kept[k, :, :more] = value[:half]
                    sent[k, :, :more] = value[half:]

    out = pl.BlockSpec((3, half, width), lambda j, places: (0, 0, j))
    shape = jax.ShapeDtypeStruct((3, half, count * UNIT + more), BF16)
    work = rows * d_cols * count * UNIT
    extras = [] if extra is None else [extra]
    return pl.pallas_call(
        kernel,
        grid_spec=pltpu.PrefetchScalarGridSpec(
            num_scalar_prefetch=1,
            grid=(steps + (more > 0),),
            in_specs=[ANY] * 5
            + [pl.BlockSpec(e.shape, lambda j, places: (0, 0)) for e in extras]
            + [ANY] * len(after),
            out_specs=[out, out],
            scratch_shapes=[
                pltpu.VMEM((2, rows, d_cols), BF16),
                pltpu.VMEM((3, 2, width, d_cols), BF16),
                pltpu.SemaphoreType.DMA((2, n)),
                pltpu.SemaphoreType.DMA((3, 2)),
            ],
        ),
        out_shape=[shape, shape],
        compiler_params=params(),
        cost_estimate=pl.CostEstimate(
            flops=6 * work, bytes_accessed=6 * d_cols * count * UNIT, transcendentals=0
        ),
        name="partial_sums",
    )(places, tokens, cotangent, w_gate, w_up, w_down, *extras, *after)


def pair_sum(kept, received, b, block, after):
    width = kept.shape[2]

    def kernel(mine, other, *rest):
        rest[-1][...] = (mine[...].astype(F32) + other[...].astype(F32)).astype(BF16)

    spec = pl.BlockSpec((3, block, width), lambda j: (0, b, 0))
    return pl.pallas_call(
        kernel,
        grid=(1,),
        in_specs=[spec, spec] + [ANY] * len(after),
        out_specs=pl.BlockSpec((3, block, width), lambda j: (0, 0, 0)),
        out_shape=jax.ShapeDtypeStruct((3, block, width), BF16),
        compiler_params=params(),
        cost_estimate=pl.CostEstimate(
            flops=3 * block * width, bytes_accessed=18 * block * width, transcendentals=0
        ),
        name="pair_sum",
    )(kept, received, *after)


def hidden_gradients(kept, received, others, width, block, after, extra=None):
    full = kept.shape[2]
    more = 0 if extra is None else extra.shape[1]

    def kernel(mine, other, *rest):
        rest, outs = rest[:-outputs], rest[-outputs:]

        def total(k, columns):
            value = mine[k, :, columns].astype(F32) + other[k, :, columns].astype(F32)
            for ref in rest[: len(others)]:
                value = value + ref[k, :, columns].astype(F32)
            return value

        for start in range(0, width, UNIT):
            columns = slice(start, start + UNIT)
            gate_pre, up_pre, back = (total(k, columns) for k in range(3))
            sig = jax.nn.sigmoid(gate_pre)
            scaled = back * sig
            grad = scaled * up_pre * (1.0 + gate_pre * (1.0 - sig))
            outs[0][0, :, columns] = grad.astype(BF16)
            outs[0][1, :, columns] = (scaled * gate_pre).astype(BF16)
        if full > width:
            outs[1][...] = total(0, slice(width, full)).astype(BF16)
        if more:
            outs[0][0, :, width:] = rest[len(others)][...]
            outs[0][1, :, width:] = jnp.zeros((block, more), BF16)

    outputs = 1 + (full > width)
    spec = pl.BlockSpec((3, block, full), lambda j: (0, 0, 0))
    small = pl.BlockSpec((block, max(full - width, more)), lambda j: (0, 0))
    extras = [] if extra is None else [extra]
    out = pl.pallas_call(
        kernel,
        grid=(1,),
        in_specs=[spec] * (2 + len(others)) + [small] * len(extras) + [ANY] * len(after),
        out_specs=[pl.BlockSpec((2, block, width + more), lambda j: (0, 0, 0)), small][:outputs],
        out_shape=[
            jax.ShapeDtypeStruct((2, block, width + more), BF16),
            jax.ShapeDtypeStruct((block, full - width), BF16),
        ][:outputs],
        compiler_params=params(),
        cost_estimate=pl.CostEstimate(
            flops=20 * block * width, bytes_accessed=22 * block * width,
            transcendentals=block * width,
        ),
        name="hidden_gradients",
    )(kept, received, *others, *extras, *after)
    return out if outputs > 1 else out[0]


def products(parts, w_gate, w_up, total, span, after, places=None, codes=None, factor=None):
    _, count = span
    hidden, d_cols = w_gate.shape
    block = parts[0].shape[1]
    n = len(parts)
    rows = block * n
    width = step_units(span, min(4, max(count // 2, 1))) * UNIT
    steps = count * UNIT // width
    before = [] if total is None else [total]
    extras = [] if codes is None else [codes, factor]
    picks = 0 if places is None else places.shape[0]

    def kernel(*refs):
        if picks:
            places, refs = refs[0], refs[1:]
        grads, weights, refs = refs[:n], refs[n : n + 2], refs[n + 2 :]
        if picks:
            outs, value_ref, buffers, sems = refs[-3 - picks : -3], *refs[-3:]
        else:
            value_ref, buffers, sems = refs[-3:]
        step = pl.program_id(0)
        start, wait, valid = tile_copies(hidden, span, width, weights, buffers, sems)

        @pl.when(step == 0)
        def _():
            start(0, 0)
            start(1, 0)
            value_ref[...] = refs[0][...] if before else jnp.zeros_like(value_ref)

        pl.when(step + 1 < steps)(lambda: start(0, step + 1))
        wait(0, step)
        value = value_ref[...]
        for k in range(2):
            if k == 1:
                pl.when(step + 1 < steps)(lambda: start(1, step + 1))
                wait(1, step)
            tile = keep_valid(buffers[k, step % 2], 0, width, valid, step == steps - 1)
            left = jnp.concatenate([g[k] for g in grads], axis=0)
            value = value + jnp.dot(left, tile, preferred_element_type=F32)
        value_ref[...] = value

        if extras:

            @pl.when(step == 0)
            def _():
                code, rest = refs[len(before) : len(before) + 2]
                value_ref[...] += jnp.dot(code[...], rest[...], preferred_element_type=F32)

        if picks:

            @pl.when(step == steps - 1)
            def _():
                for k, out in enumerate(outs):
                    begin = pl.multiple_of(places[k] * block, block)
                    out[...] = value_ref[pl.ds(begin, block)].astype(out.dtype)

    grad = pl.BlockSpec((2, block, width), lambda j, *_: (0, 0, j))
    whole = pl.BlockSpec((rows, d_cols), lambda j, *_: (0, 0))
    piece = pl.BlockSpec((block, d_cols), lambda j, *_: (0, 0))
    work = rows * d_cols * count * UNIT
    in_specs = [grad] * n + [ANY, ANY] + [whole] * len(before)
    in_specs += [pl.BlockSpec(e.shape, lambda j, *_: (0, 0)) for e in extras]
    scratch = [
        pltpu.VMEM((2, 2, width, d_cols), BF16),
        pltpu.SemaphoreType.DMA((2, 2)),
    ]
    if picks:
        out_specs = [piece] * picks
        out_shape = [
            jax.ShapeDtypeStruct((block, d_cols), BF16 if k else F32) for k in range(picks)
        ]
        scratch = [pltpu.VMEM((rows, d_cols), F32)] + scratch
    else:
        out_specs = whole
        out_shape = jax.ShapeDtypeStruct((rows, d_cols), F32)
    return pl.pallas_call(
        kernel,
        grid_spec=pltpu.PrefetchScalarGridSpec(
            num_scalar_prefetch=1 if picks else 0,
            grid=(steps,),
            in_specs=in_specs + [ANY] * len(after),
            out_specs=out_specs,
            scratch_shapes=scratch,
        ),
        out_shape=out_shape,
        compiler_params=params(),
        cost_estimate=pl.CostEstimate(
            flops=4 * work, bytes_accessed=4 * d_cols * count * UNIT, transcendentals=0
        ),
        name="products",
    )(*([places] if picks else []), *parts, w_gate, w_up, *before, *extras, *after)


def ordered(value, *earlier):
    return lax.optimization_barrier((value, *earlier))[0]


def backward(tokens, cotangent, w_gate, w_up, w_down, common_down_factor, head_up, routes):
    tok_rows, d_cols = tokens.shape
    hidden = w_gate.shape[1]
    rank = common_down_factor.shape[1]
    local_heads = head_up.shape[0]
    n_tensor, n_head, n_dp = (lax.axis_size(a) for a in ("tensor", "head", "dp"))
    chips = n_tensor // 2
    me = lax.axis_index("tensor")
    my_chip, my_core = me // 2, me % 2
    my_head, my_dp = lax.axis_index("head"), lax.axis_index("dp")
    block = tok_rows // n_tensor
    out_rows = tok_rows // n_head
    if out_rows != block or n_tensor % 2:
        raise ValueError("unsupported mesh")

    def place_of(owner):
        core, chip = owner // chips, owner % chips
        return (core + my_core) % 2 * chips + (chip - my_chip) % chips

    order = jnp.arange(n_tensor, dtype=jnp.int32)
    places = (order // chips + my_core) % 2 * chips + (order % chips + my_chip) % chips

    def relative(rows):
        return jnp.concatenate(
            [
                lax.dynamic_slice_in_dim(rows, places[k] * block, block, 0)
                for k in range(n_tensor)
            ],
            axis=0,
        )

    def absolute(rows):
        return jnp.concatenate(
            [
                lax.dynamic_slice_in_dim(rows, place_of(k) * block, block, 0)
                for k in range(n_tensor)
            ],
            axis=0,
        )

    def swap_core(value):
        return lax.ppermute(value, "tensor", [(i, i ^ 1) for i in range(n_tensor)])

    def shift_chip(value, step):
        pairs = [(i, (i // 2 + step) % chips * 2 + i % 2) for i in range(n_tensor)]
        return lax.ppermute(value, "tensor", pairs)

    def shift(value, axis, count, step):
        return lax.ppermute(value, axis, [(i, (i + step) % count) for i in range(count)])

    head_ids = my_head * local_heads + jnp.arange(local_heads, dtype=jnp.int32)[None, :]

    def adapter_parts(earlier):
        own_tokens, own_cotangent = ordered(tokens, earlier), ordered(cotangent, earlier)
        codes = jnp.dot(own_tokens, common_down_factor, preferred_element_type=F32)
        separated = contract_last(
            own_cotangent, head_up.reshape(local_heads * rank, d_cols)
        )
        code_grad = ADAPTER_SCALE * jnp.sum(
            separated.reshape(tok_rows, local_heads, rank)
            * (routes == head_ids).astype(F32)[:, :, None],
            axis=1,
        )
        return relative(jnp.concatenate([codes, code_grad], axis=1).astype(BF16))

    spans = chunk_units(hidden)
    count = len(spans)
    w_gate, w_up = w_gate.T, w_up.T
    sums, grads, after = [], [], []
    adapter = {}

    def finish(c, after):
        kept, received, others = sums[c]
        own = hidden_gradients(
            kept, received, others, spans[c][1] * UNIT, block, after,
            adapter["own"] if c == 3 else None,
        )
        if c == 1:
            own, adapter["own"] = own
        near = swap_core(own)
        far = [shift_chip(own, -b) for b in range(1, chips)]
        grads.append([own] + far + [near] + [swap_core(f) for f in far])
        return own

    other_cotangents = [shift(cotangent, "dp", n_dp, s) for s in range(1, n_dp)]

    for c, span in enumerate(spans):
        kept, sent = partial_sums(
            places, tokens, cotangent, w_gate, w_up, w_down, span, after,
            adapter["part"] if c == 1 else None,
        )
        received = swap_core(sent)
        after = [kept]
        if c == 0:
            adapter["part"] = adapter_parts(kept)
            after = [adapter["part"]]
        if c >= 2:
            after = [finish(c - 2, after)]
        pairs = [pair_sum(kept, received, b, block, after) for b in range(1, chips)]
        others = [shift_chip(p, b + 1) for b, p in enumerate(pairs)]
        sums.append((kept, received, others))
        after = pairs[-1:]

    rows = None
    head_places = place_of((my_head + jnp.arange(n_head, dtype=jnp.int32)) % n_head)
    for c, span in enumerate(spans):
        extra = {}
        if c == 3:
            start = span[1] * UNIT
            adapter["all"] = jnp.concatenate([g[0, :, start:] for g in grads[c]], axis=0)
            extra = dict(codes=adapter["all"][:, rank:], factor=common_down_factor.T)
        rows = products(
            grads[c], w_gate, w_up, rows, span, after,
            head_places if c == count - 1 else None, **extra,
        )
        if c == count - 1:
            break
        after = [rows]
        if len(grads) < count:
            after = [finish(len(grads), after)]
        if c == 3:
            both = absolute(ordered(adapter["all"], rows))
            codes = jnp.concatenate([both[:, :rank], routes.astype(BF16)], axis=1)
            other_codes = [shift(codes, "dp", n_dp, s) for s in range(1, n_dp)]
            part = both[:, rank:]
            head_parts = [shift(part, "head", n_head, s) for s in range(1, n_head)]
            after = after + [codes, part]

    def by_group(own, others):
        doubled = jnp.concatenate([own] + others[::-1], axis=0)
        doubled = jnp.concatenate([doubled, doubled], axis=0)
        count = own.shape[0]
        start = (n_dp - my_dp) % n_dp * count
        return lax.dynamic_slice_in_dim(doubled, start, n_dp * count, 0)

    received = [shift(rows[s], "head", n_head, s) for s in range(1, n_head)]

    code_grad = ordered(part, rows[0]).astype(F32)
    for other in head_parts:
        code_grad = code_grad + other.astype(F32)
    code_grad = code_grad.astype(BF16)
    shared = contract_first(code_grad, tokens)
    grad_shared = shared
    for s in range(1, n_dp):
        grad_shared = grad_shared + shift(shared, "dp", n_dp, s)
    grad_shared = grad_shared.T

    all_codes = by_group(ordered(codes, rows[0], shared), other_codes)
    all_cotangents = by_group(ordered(cotangent, rows[0], shared), other_cotangents)
    masked = jnp.where(
        (all_codes[:, rank:].astype(jnp.int32) == head_ids)[:, :, None],
        all_codes[:, None, :rank],
        jnp.zeros((), BF16),
    ).reshape(n_dp * tok_rows, local_heads * rank)
    up_heads = ADAPTER_SCALE * contract_first(masked, all_cotangents)
    up_heads = up_heads.reshape(local_heads, rank, d_cols)

    grad_x = rows[0]
    for other in received:
        grad_x = grad_x + other.astype(F32)
    return grad_x.astype(BF16), grad_shared, up_heads


def solution(mesh):
    placed = (
        P("dp", "tensor"),
        P("dp", "tensor"),
        P("tensor", "head"),
        P("tensor", "head"),
        P("head", "tensor"),
        P("tensor", None),
        P("head", None, "tensor"),
        P("dp", None),
    )
    return jax.shard_map(
        backward,
        mesh=mesh,
        in_specs=placed,
        out_specs=(P(("dp", "head"), "tensor"), P("tensor", None), P("head", None, "tensor")),
        check_vma=False,
    )
```

```python
import jax
import jax.numpy as jnp
from jax import lax
from jax.experimental import pallas as pl
from jax.experimental.pallas import tpu as pltpu
from jax.sharding import PartitionSpec as P


ADAPTER_SCALE = 2.0
SHARES = (5, 6, 8, 6, 4)
UNIT = 256
F32, BF16 = jnp.float32, jnp.bfloat16
ANY = pl.BlockSpec(memory_space=pl.ANY)


def contract_last(left, right):
    return lax.dot_general(
        left, right, (((1,), (1,)), ((), ())), preferred_element_type=F32
    )


def contract_first(left, right):
    return lax.dot_general(
        left, right, (((0,), (0,)), ((), ())), preferred_element_type=F32
    )


def chunk_units(hidden):
    units = pl.cdiv(hidden, UNIT)
    total, spans, left, seen = sum(SHARES), [], units, 0
    for share in SHARES:
        seen += share
        first = units - units * seen // total
        if first < left:
            spans.append((first, left - first))
        left = min(left, first)
    return spans


def params(limit_mib=22):
    return pltpu.CompilerParams(vmem_limit_bytes=limit_mib * 2**20)


def token_shape():
    return jax.ShapeDtypeStruct((8, 128), F32)


def keep_valid(value, axis, valid):
    unit = lax.broadcasted_iota(jnp.int32, value.shape, axis)
    return jnp.where(unit < valid, value, jnp.zeros_like(value))


def partial_sums(places, tokens, cotangent, w_gate, w_up, w_down, span, after, extra=None, limit=22):
    first, count = span
    rows, d_cols = tokens.shape
    hidden = w_gate.shape[0]
    half, n = rows // 2, places.shape[0]
    block = rows // n
    width = 2 * UNIT
    steps = pl.cdiv(count, 2)
    more = 0 if extra is None else extra.shape[1]
    last_units = min(hidden - (first + count - 1) * UNIT, UNIT)

    def kernel(places, *refs):
        sides, weights, refs = refs[:2], refs[2:5], refs[5:]
        kept, sent, token, held, buffers, row_sems, sems = refs[-7:]
        step = pl.program_id(0)

        def row_copy(side, k):
            origin = pl.multiple_of(places[k] * block, block)
            return pltpu.make_async_copy(
                sides[side].at[pl.ds(origin, block)],
                held.at[side, pl.ds(k * block, block)],
                row_sems.at[side, k],
            )

        def piece(k, at, u, use):
            def run(units):
                origin = pl.multiple_of((first + 2 * at + u) * UNIT, UNIT)
                use(
                    pltpu.make_async_copy(
                        weights[k].at[pl.ds(origin, units)],
                        buffers.at[k, at % 2, pl.ds(u * UNIT, units)],
                        sems.at[k, at % 2, u],
                    )
                )

            final = (count - 1) // 2, (count - 1) % 2
            if last_units == UNIT and (u == 0 or count % 2 == 0):
                run(UNIT)
                return
            pl.when(at < steps - 1)(lambda: run(UNIT))
            if u <= final[1]:
                pl.when(at == steps - 1)(lambda: run(last_units if u == final[1] else UNIT))

        def start(k, at, u):
            piece(k, at, u, lambda copy: copy.start())

        def wait(k, at, u):
            piece(k, at, u, lambda copy: copy.wait())

        @pl.when(step == 0)
        def _():
            start(0, 0, 0)
            for k in range(n):
                row_copy(0, k).start()
            start(0, 0, 1)
            start(1, 0, 0)
            start(1, 0, 1)
            for k in range(n):
                row_copy(1, k).start()
            start(2, 0, 0)
            start(2, 0, 1)
            for k in range(n):
                row_copy(0, k).wait()

        @pl.when(step < steps)
        def _():
            for k in range(3):

                @pl.when(step + 1 < steps)
                def _():
                    start(k, step + 1, 0)
                    start(k, step + 1, 1)

                if k == 2:

                    @pl.when(step == 0)
                    def _():
                        for b in range(n):
                            row_copy(1, b).wait()

                wait(k, step, 0)
                wait(k, step, 1)
                part = contract_last(held[k // 2], buffers[k, step % 2])
                if last_units < UNIT or count % 2:
                    valid = (count - 1 - 2 * step) * UNIT + last_units
                    part = keep_valid(part, 1, valid)
                kept[k] = part[:half].astype(BF16)
                sent[k] = part[half:].astype(BF16)
            token[...] = jnp.zeros_like(token)

        if more:

            @pl.when(step == count // 2)
            def _():
                columns = slice(count % 2 * UNIT, count % 2 * UNIT + more)
                for k in range(n):
                    origin = pl.multiple_of(places[k] * block, block)
                    out, row = (kept, k) if k < n // 2 else (sent, k - n // 2)
                    at = slice(row * block, (row + 1) * block)
                    out[0, at, columns] = refs[0][pl.ds(origin, block)]
                for out in (kept, sent):
                    out[1:, :, columns] = jnp.zeros((2, half, more), BF16)

    out = pl.BlockSpec((3, half, width), lambda j, places: (0, 0, j))
    shape = jax.ShapeDtypeStruct((3, half, count * UNIT + more), BF16)
    work = rows * d_cols * count * UNIT
    extras = [] if extra is None else [extra]
    return pl.pallas_call(
        kernel,
        grid_spec=pltpu.PrefetchScalarGridSpec(
            num_scalar_prefetch=1,
            grid=(steps + (more > 0 and count % 2 == 0),),
            in_specs=[ANY] * 5
            + [pl.BlockSpec(e.shape, lambda j, places: (0, 0)) for e in extras]
            + [ANY] * len(after),
            out_specs=[out, out, pl.BlockSpec((8, 128), lambda j, places: (0, 0))],
            scratch_shapes=[
                pltpu.VMEM((2, rows, d_cols), BF16),
                pltpu.VMEM((3, 2, width, d_cols), BF16),
                pltpu.SemaphoreType.DMA((2, n)),
                pltpu.SemaphoreType.DMA((3, 2, 2)),
            ],
        ),
        out_shape=[shape, shape, token_shape()],
        compiler_params=params(limit),
        cost_estimate=pl.CostEstimate(
            flops=6 * work, bytes_accessed=6 * d_cols * count * UNIT, transcendentals=0
        ),
        name="partial_sums",
    )(places, tokens, cotangent, w_gate, w_up, w_down, *extras, *after)


def fetch(sources, buffers, sems):
    copies = [
        pltpu.make_async_copy(source, buffers.at[k], sems.at[k])
        for k, source in enumerate(sources)
    ]
    for copy in copies:
        copy.start()
    for copy in copies:
        copy.wait()


def pair_sum(kept, received, b, block, after):
    width = kept.shape[2]
    rows = pl.ds(b * block, block)

    def kernel(mine, other, *rest):
        out, token, buffers, sems = rest[-4:]
        token[...] = jnp.zeros_like(token)
        fetch([mine.at[:, rows], other.at[:, rows]], buffers, sems)
        out[...] = (buffers[0].astype(F32) + buffers[1].astype(F32)).astype(BF16)

    return pl.pallas_call(
        kernel,
        in_specs=[ANY] * (2 + len(after)),
        out_specs=[pl.BlockSpec(memory_space=pltpu.VMEM)] * 2,
        out_shape=[jax.ShapeDtypeStruct((3, block, width), BF16), token_shape()],
        scratch_shapes=[
            pltpu.VMEM((2, 3, block, width), BF16),
            pltpu.SemaphoreType.DMA((2,)),
        ],
        compiler_params=params(),
        cost_estimate=pl.CostEstimate(
            flops=3 * block * width, bytes_accessed=18 * block * width, transcendentals=0
        ),
        name="pair_sum",
    )(kept, received, *after)


def hidden_gradients(kept, received, others, width, block, after, extra=None):
    full = kept.shape[2]
    more = 0 if extra is None else extra.shape[1]
    parts = 2 + len(others)
    outputs = 1 + (full > width)
    extras = [] if extra is None else [extra]

    def kernel(*refs):
        outs, (token, buffers, sems) = refs[-3 - outputs : -3], refs[-3:]
        token[...] = jnp.zeros_like(token)
        mine = pl.ds(0, block)
        fetch(
            [refs[0].at[:, mine], refs[1].at[:, mine], *refs[2:parts]], buffers, sems
        )

        def total(k, columns):
            value = buffers[0, k, :, columns].astype(F32)
            for part in range(1, parts):
                value = value + buffers[part, k, :, columns].astype(F32)
            return value

        for start in range(0, width, UNIT):
            columns = slice(start, start + UNIT)
            gate_pre, up_pre, back = (total(k, columns) for k in range(3))
            sig = jax.nn.sigmoid(gate_pre)
            scaled = back * sig
            grad = scaled * up_pre * (1.0 + gate_pre * (1.0 - sig))
            outs[0][0, :, columns] = grad.astype(BF16)
            outs[0][1, :, columns] = (scaled * gate_pre).astype(BF16)
        if full > width:
            outs[1][...] = total(0, slice(width, full)).astype(BF16)
        if more:
            outs[0][0, :, width:] = refs[parts][...]
            outs[0][1, :, width:] = jnp.zeros((block, more), BF16)

    vmem = pl.BlockSpec(memory_space=pltpu.VMEM)
    return pl.pallas_call(
        kernel,
        in_specs=[ANY] * parts + [vmem] * len(extras) + [ANY] * len(after),
        out_specs=[vmem] * (outputs + 1),
        out_shape=[
            jax.ShapeDtypeStruct((2, block, width + more), BF16),
            jax.ShapeDtypeStruct((block, full - width), BF16),
        ][:outputs]
        + [token_shape()],
        scratch_shapes=[
            pltpu.VMEM((parts, 3, block, full), BF16),
            pltpu.SemaphoreType.DMA((parts,)),
        ],
        compiler_params=params(),
        cost_estimate=pl.CostEstimate(
            flops=20 * block * width, bytes_accessed=22 * block * width,
            transcendentals=block * width,
        ),
        name="hidden_gradients",
    )(kept, received, *others, *extras, *after)


def products(groups, w_gate, w_up, total, after, columns, places=None, factor=None):
    left, wide = columns
    hidden = w_gate.shape[0]
    n = len(groups[0][1])
    block = groups[0][1][0].shape[1]
    rows = block * n
    step_units = 2 if all(span[1] % 2 == 0 for span, _ in groups) else 1
    width = step_units * UNIT
    bounds = [0]
    for span, _ in groups:
        bounds.append(bounds[-1] + span[1] // step_units)
    steps = bounds[-1]
    ragged = [
        min(hidden - (span[0] + span[1]) * UNIT + width, width) for span, _ in groups
    ]
    picks = 0 if places is None else places.shape[0]
    more = 0 if factor is None else factor.shape[0]
    before = [] if total is None else [total]
    factors = [] if factor is None else [factor]

    def kernel(*refs):
        if picks:
            places, refs = refs[0], refs[1:]
        parts = [refs[n * g : n * (g + 1)] for g in range(len(groups))]
        refs = refs[n * len(groups) :]
        weights, refs = refs[:2], refs[2:]
        value, tiles, grads, codes_buffer, tile_sems, grad_sems, sems = refs[-7:]
        outs = refs[: -7][len(before) + len(factors) + len(after) :]
        step = pl.program_id(0)

        def in_group(at, use):
            for g, (span, _) in enumerate(groups):
                local = at - bounds[g]
                inside = jnp.logical_and(at >= bounds[g], at < bounds[g + 1])
                if ragged[g] == width:
                    pl.when(inside)(lambda: use(g, local, width))
                else:
                    is_last = at == bounds[g + 1] - 1
                    pl.when(jnp.logical_and(inside, is_last))(
                        lambda: use(g, local, ragged[g])
                    )
                    pl.when(jnp.logical_and(inside, jnp.logical_not(is_last)))(
                        lambda: use(g, local, width)
                    )

        def tile(k, at, act):
            def use(g, local, units):
                origin = pl.multiple_of(groups[g][0][0] * UNIT + local * width, UNIT)
                act(
                    pltpu.make_async_copy(
                        weights[k].at[pl.ds(origin, units), pl.ds(left, wide)],
                        tiles.at[k, at % 2, pl.ds(0, units)],
                        tile_sems.at[k, at % 2],
                    )
                )

            in_group(at, use)

        def gradient(at, act):
            def use(g, local, units):
                origin = pl.multiple_of(local * width, UNIT)
                for p in range(n):
                    act(
                        pltpu.make_async_copy(
                            parts[g][p].at[:, :, pl.ds(origin, width)],
                            grads.at[at % 2, :, pl.ds(p * block, block)],
                            grad_sems.at[at % 2, p],
                        )
                    )

            in_group(at, use)

        def begin(copy):
            copy.start()

        def end(copy):
            copy.wait()

        def code_copy(p):
            origin = groups[0][0][1] * UNIT
            return pltpu.make_async_copy(
                parts[0][p].at[0, :, pl.ds(origin, more)],
                codes_buffer.at[pl.ds(p * block, block)],
                sems.at[p],
            )

        def total_copy():
            return pltpu.make_async_copy(
                refs[0].at[:, pl.ds(left, wide)], value, sems.at[n]
            )

        @pl.when(step == 0)
        def _():
            gradient(0, begin)
            tile(0, 0, begin)
            if before:
                total_copy().start()
            tile(1, 0, begin)
            if more:
                for p in range(n):
                    code_copy(p).start()
            if before:
                total_copy().wait()
            else:
                value[...] = jnp.zeros_like(value)

        @pl.when(step + 1 < steps)
        def _():
            gradient(step + 1, begin)
            tile(0, step + 1, begin)

        gradient(step, end)
        result = value[...]
        for k in range(2):
            if k == 1:
                pl.when(step + 1 < steps)(lambda: tile(1, step + 1, begin))
            tile(k, step, end)
            part = tiles[k, step % 2]
            if any(r < width for r in ragged):
                valid = jnp.int32(width)
                for g, r in enumerate(ragged):
                    valid = jnp.where(step == bounds[g + 1] - 1, r, valid)
                part = keep_valid(part, 0, valid)
            result = result + jnp.dot(
                grads[step % 2, k], part, preferred_element_type=F32
            )
        value[...] = result

        if more:

            @pl.when(step == steps - 1)
            def _():
                for p in range(n):
                    code_copy(p).wait()
                outs[-1][...] = codes_buffer[...]
                value[...] += jnp.dot(
                    codes_buffer[...], refs[len(before)][:, left : left + wide],
                    preferred_element_type=F32,
                )

        @pl.when(step == steps - 1)
        def _():
            outs[0][...] = jnp.zeros_like(outs[0])
            if picks:
                for k in range(picks):
                    origin = pl.multiple_of(places[k] * block, block)
                    out = outs[1 + k]
                    out[...] = value[pl.ds(origin, block)].astype(out.dtype)
            else:
                outs[1][...] = value[...]

    def whole(shape):
        return pl.BlockSpec(shape, lambda j, *_: (0,) * len(shape))

    work = rows * wide * steps * width
    if picks:
        out_shape = [
            jax.ShapeDtypeStruct((block, wide), BF16 if k else F32) for k in range(picks)
        ]
    else:
        out_shape = [jax.ShapeDtypeStruct((rows, wide), F32)]
    out_shape = [token_shape()] + out_shape
    if more:
        out_shape = out_shape + [jax.ShapeDtypeStruct((rows, more), BF16)]
    flat = [part for _, parts in groups for part in parts]
    return pl.pallas_call(
        kernel,
        grid_spec=pltpu.PrefetchScalarGridSpec(
            num_scalar_prefetch=1 if picks else 0,
            grid=(steps,),
            in_specs=[ANY] * (len(flat) + 2 + len(before))
            + [whole(f.shape) for f in factors]
            + [ANY] * len(after),
            out_specs=[whole(shape.shape) for shape in out_shape],
            scratch_shapes=[
                pltpu.VMEM((rows, wide), F32),
                pltpu.VMEM((2, 2, width, wide), BF16),
                pltpu.VMEM((2, 2, rows, width), BF16),
                pltpu.VMEM((rows, max(more, 128)), BF16),
                pltpu.SemaphoreType.DMA((2, 2)),
                pltpu.SemaphoreType.DMA((2, n)),
                pltpu.SemaphoreType.DMA((n + 1,)),
            ],
        ),
        out_shape=out_shape,
        compiler_params=params(),
        cost_estimate=pl.CostEstimate(
            flops=4 * work, bytes_accessed=4 * wide * steps * width, transcendentals=0
        ),
        name="products",
    )(*([places] if picks else []), *flat, w_gate, w_up, *before, *factors, *after)


def adapter_columns(tokens, cotangent, factor, heads, places, after):
    rows, d_cols = tokens.shape
    rank = factor.shape[0]
    width = min(4 * rank, heads.shape[0])
    steps = heads.shape[0] // width

    def kernel(tok, cot, down, up, head, *rest):
        out, token, total = rest[-3:]
        step = pl.program_id(0)

        @pl.when(step == 0)
        def _():
            token[...] = jnp.zeros_like(token)
            total[...] = jnp.zeros_like(total)
            out[:, :rank] = contract_last(tok[...], down[...]).astype(BF16)

        separated = contract_last(cot[...], up[...])
        column = lax.broadcasted_iota(jnp.int32, separated.shape, 1)
        chosen = step * (width // rank) + column // rank == head[...]
        part = jnp.where(chosen, ADAPTER_SCALE * separated, 0.0).astype(BF16)
        row = lax.broadcasted_iota(jnp.int32, (width, rank), 0)
        fold = row % rank == lax.broadcasted_iota(jnp.int32, (width, rank), 1)
        total[...] += jnp.dot(part, fold.astype(BF16), preferred_element_type=F32)

        @pl.when(step == steps - 1)
        def _():
            out[:, rank:] = total[...].astype(BF16)

    def whole(shape):
        return pl.BlockSpec(shape, lambda j: (0, 0))

    return pl.pallas_call(
        kernel,
        grid=(steps,),
        in_specs=[
            whole(tokens.shape),
            whole(tokens.shape),
            whole(factor.shape),
            pl.BlockSpec((width, d_cols), lambda j: (j, 0)),
            whole(places.shape),
        ]
        + [ANY] * len(after),
        out_specs=[whole((rows, 2 * rank)), whole((8, 128))],
        out_shape=[jax.ShapeDtypeStruct((rows, 2 * rank), BF16), token_shape()],
        scratch_shapes=[pltpu.VMEM((rows, rank), F32)],
        compiler_params=params(),
        cost_estimate=pl.CostEstimate(
            flops=2 * rows * d_cols * (rank + heads.shape[0]),
            bytes_accessed=2 * d_cols * heads.shape[0],
            transcendentals=0,
        ),
        name="adapter_columns",
    )(tokens, cotangent, factor, heads, places, *after)


def gather_columns(places, parts, start, after):
    n, block = len(parts), parts[0].shape[1]
    more = parts[0].shape[2] - start

    def kernel(places, *refs):
        out, token, buffer, sems = refs[-4:]
        token[...] = jnp.zeros_like(token)
        copies = [
            pltpu.make_async_copy(
                refs[k].at[0, :, pl.ds(start, more)], buffer.at[k], sems.at[k]
            )
            for k in range(n)
        ]
        for copy in copies:
            copy.start()
        for copy in copies:
            copy.wait()
        for k in range(n):
            origin = pl.multiple_of(places[k] * block, block)
            out[pl.ds(origin, block)] = buffer[k]

    shape = jax.ShapeDtypeStruct((n * block, more), BF16)
    return pl.pallas_call(
        kernel,
        grid_spec=pltpu.PrefetchScalarGridSpec(
            num_scalar_prefetch=1,
            grid=(1,),
            in_specs=[ANY] * (n + len(after)),
            out_specs=[
                pl.BlockSpec(shape.shape, lambda j, places: (0, 0)),
                pl.BlockSpec((8, 128), lambda j, places: (0, 0)),
            ],
            scratch_shapes=[
                pltpu.VMEM((n, block, more), BF16),
                pltpu.SemaphoreType.DMA((n,)),
            ],
        ),
        out_shape=[shape, token_shape()],
        compiler_params=params(),
        name="gather_columns",
    )(places, *parts, *after)


def ordered(value, *earlier):
    return lax.optimization_barrier((value, *earlier))[0]


def backward(tokens, cotangent, w_gate, w_up, w_down, common_down_factor, head_up, routes):
    tok_rows, d_cols = tokens.shape
    hidden = w_gate.shape[1]
    rank = common_down_factor.shape[1]
    local_heads = head_up.shape[0]
    n_tensor, n_head, n_dp = (lax.axis_size(a) for a in ("tensor", "head", "dp"))
    chips = n_tensor // 2
    me = lax.axis_index("tensor")
    my_chip, my_core = me // 2, me % 2
    my_head, my_dp = lax.axis_index("head"), lax.axis_index("dp")
    block = tok_rows // n_tensor
    out_rows = tok_rows // n_head
    if out_rows != block or n_tensor % 2:
        raise ValueError("unsupported mesh")

    def place_of(owner):
        core, chip = owner // chips, owner % chips
        return (core + my_core) % 2 * chips + (chip - my_chip) % chips

    order = jnp.arange(n_tensor, dtype=jnp.int32)
    places = (order // chips + my_core) % 2 * chips + (order % chips + my_chip) % chips

    def swap_core(value):
        return lax.ppermute(value, "tensor", [(i, i ^ 1) for i in range(n_tensor)])

    def shift_chip(value, step):
        pairs = [(i, (i // 2 + step) % chips * 2 + i % 2) for i in range(n_tensor)]
        return lax.ppermute(value, "tensor", pairs)

    def shift(value, axis, count, step):
        return lax.ppermute(value, axis, [(i, (i + step) % count) for i in range(count)])

    head_ids = my_head * local_heads + jnp.arange(local_heads, dtype=jnp.int32)[None, :]

    spans = chunk_units(hidden)
    count = len(spans)
    w_gate, w_up = w_gate.T, w_up.T
    sums, grads, after = [], [], []
    adapter = {}

    def finish(c, after):
        kept, received, others = sums[c]
        own, *rest, token = hidden_gradients(
            kept, received, others, spans[c][1] * UNIT, block, after,
            adapter["own"] if c == 2 else None,
        )
        if c == 1:
            adapter["own"] = rest[0]
        near = swap_core(own)
        far = [shift_chip(own, -b) for b in range(1, chips)]
        grads.append([own] + far + [near] + [swap_core(f) for f in far])
        return token

    other_cotangents = [shift(cotangent, "dp", n_dp, s) for s in range(1, n_dp)]

    for c, span in enumerate(spans):
        kept, sent, token = partial_sums(
            places, tokens, cotangent, w_gate, w_up, w_down, span, after,
            adapter["part"] if c == 1 else None, 60 if c == 0 else 22,
        )
        received = swap_core(sent)
        after = [token]
        if c == 0:
            adapter["part"], token = adapter_columns(
                tokens, cotangent, common_down_factor.T,
                head_up.reshape(local_heads * rank, d_cols),
                routes - my_head * local_heads, after,
            )
            after = [token]
        if c >= 2:
            after = [finish(c - 2, after)]
        pairs = [pair_sum(kept, received, b, block, after) for b in range(1, chips)]
        others = [shift_chip(p, b + 1) for b, (p, _) in enumerate(pairs)]
        sums.append((kept, received, others))
        after = [token for _, token in pairs]

    total = None
    head_places = place_of((my_head + jnp.arange(n_head, dtype=jnp.int32)) % n_head)
    for c in range(count - 2):
        token, total = products(
            [(spans[c], grads[c])], w_gate, w_up, total, after, (0, d_cols)
        )
        after = [token]
        if c >= count - 4:
            after = [finish(len(grads), after)]

    both, token = gather_columns(places, grads[2], spans[2][1] * UNIT, after)
    after = [token]
    codes = jnp.concatenate([both[:, :rank], routes.astype(BF16)], axis=1)
    part = both[:, rank:]
    other_codes = [shift(codes, "dp", n_dp, s) for s in range(1, n_dp)]
    head_parts = [shift(part, "head", n_head, s) for s in range(1, n_head)]

    code_grad = ordered(part, token).astype(F32)
    for other in head_parts:
        code_grad = code_grad + other.astype(F32)
    code_grad = code_grad.astype(BF16)
    shared = contract_first(code_grad, tokens)
    other_shared = [shift(shared, "dp", n_dp, s) for s in range(1, n_dp)]

    own_rows, received = [], []
    wide = d_cols // 2
    for side in range(2):
        token, own, *sends = products(
            list(zip(spans[-2:], grads[-2:])), w_gate, w_up, total, after,
            (side * wide, wide), head_places,
        )
        after = [token]
        own_rows.append(own)
        received.append(
            [shift(send, "head", n_head, s + 1) for s, send in enumerate(sends)]
        )

    def by_group(own, others):
        doubled = jnp.concatenate([own] + others[::-1], axis=0)
        doubled = jnp.concatenate([doubled, doubled], axis=0)
        count = own.shape[0]
        start = (n_dp - my_dp) % n_dp * count
        return lax.dynamic_slice_in_dim(doubled, start, n_dp * count, 0)

    all_codes = by_group(ordered(codes, token), other_codes)
    all_cotangents = by_group(ordered(cotangent, token), other_cotangents)
    masked = jnp.where(
        (all_codes[:, rank:].astype(jnp.int32) == head_ids)[:, :, None],
        all_codes[:, None, :rank],
        jnp.zeros((), BF16),
    ).reshape(n_dp * tok_rows, local_heads * rank)
    up_heads = ADAPTER_SCALE * contract_first(masked, all_cotangents)
    up_heads = up_heads.reshape(local_heads, rank, d_cols)

    grad_shared = ordered(shared, token)
    for other in other_shared:
        grad_shared = grad_shared + other
    grad_shared = grad_shared.T

    own_code_grad = lax.dynamic_slice_in_dim(code_grad, my_head * out_rows, out_rows, 0)
    adapter_rows = contract_last(own_code_grad, common_down_factor)
    halves = []
    for side, (own, others) in enumerate(zip(own_rows, received)):
        own = own + adapter_rows[:, side * wide : (side + 1) * wide]
        for other in others:
            own = own + other.astype(F32)
        halves.append(own.astype(BF16))
    return jnp.concatenate(halves, axis=1), grad_shared, up_heads


def solution(mesh):
    placed = (
        P("dp", "tensor"),
        P("dp", "tensor"),
        P("tensor", "head"),
        P("tensor", "head"),
        P("head", "tensor"),
        P("tensor", None),
        P("head", None, "tensor"),
        P("dp", None),
    )
    return jax.shard_map(
        backward,
        mesh=mesh,
        in_specs=placed,
        out_specs=(P(("dp", "head"), "tensor"), P("tensor", None), P("head", None, "tensor")),
        check_vma=False,
    )
```
